32 devices in a mesh: dp: 16 (over z, y, x), tensor: 2 (over core).
Axes of the slice: x: 2, y: 2, z: 4, core: 2. Of those that a mesh axis runs over, the one named last changes fastest.
Arguments:
- tokens: bfloat16 [1024, 16, 2560], P('tensor', 'dp'), may hold values from -6 to 6
- pre_gain: float32 [2560], replicated, may hold values from 0.25 to 1.75
- z_weight: bfloat16 [2560, 5120], P(None, 'tensor'), may hold values from -0.125 to 0.125
- x_weight: bfloat16 [2560, 5120], P(None, 'tensor'), may hold values from -0.125 to 0.125
- bc_weight: bfloat16 [2560, 256], replicated, may hold values from -0.125 to 0.125
- dt_weight: bfloat16 [2560, 80], P(None, 'tensor'), may hold values from -0.125 to 0.125
- conv_x_weight: float32 [4, 5120], P(None, 'tensor'), may hold values from -3 to 3
- conv_x_bias: float32 [5120], P('tensor'), may hold values from -3 to 3
- conv_bc_weight: float32 [4, 256], replicated, may hold values from -3 to 3
- conv_bc_bias: float32 [256], replicated, may hold values from -3 to 3
- dt_bias: float32 [80], P('tensor'), may hold values from -4 to -2
- decay_log: float32 [80], P('tensor'), may hold values from -6 to 0
- skip_gain: float32 [80], P('tensor'), may hold values from 0.5 to 2
- norm_gain: float32 [5120], P('tensor'), may hold values from 0.25 to 1.75
- out_weight: bfloat16 [5120, 2560], P('tensor'), may hold values from -0.078125 to 0.078125
- cotangent: bfloat16 [1024, 16, 2560], P('tensor', 'dp'), may hold values from -6 to 6
Outputs:
- layer_out: bfloat16 [1024, 16, 2560], P('tensor', 'dp')
- grad_tokens: bfloat16 [1024, 16, 2560], P('tensor', 'dp')
- grad_pre_gain: float32 [2560], replicated
- grad_z_weight: float32 [2560, 5120], P('dp', 'tensor')
- grad_x_weight: float32 [2560, 5120], P('dp', 'tensor')
- grad_bc_weight: float32 [2560, 256], P('dp')
- grad_dt_weight: float32 [2560, 80], P('dp', 'tensor')
- grad_conv_x_weight: float32 [4, 5120], P(None, 'tensor')
- grad_conv_x_bias: float32 [5120], P('tensor')
- grad_conv_bc_weight: float32 [4, 256], replicated
- grad_conv_bc_bias: float32 [256], replicated
- grad_dt_bias: float32 [80], P('tensor')
- grad_decay_log: float32 [80], P('tensor')
- grad_skip_gain: float32 [80], P('tensor')
- grad_norm_gain: float32 [5120], P('tensor')
- grad_out_weight: float32 [5120, 2560], P('tensor', 'dp')
The draws below stay inside these ranges and needn't reach their ends.
All inputs are finite; a program needn't handle non-finite values.
Results may differ from the reference program's by a relative error of at most 0.012.
The reference program's roundings to bfloat16 on the way (of `normed` and `gated`) count: a program that leaves them out, or rounds other values in their place, can miss the bound.
Values may be sent and summed in bfloat16 or wider, within the bound.
A program may use at most 384 MiB of HBM per device.

```python
import jax
import jax.numpy as jnp
from jax import lax

D = 2560
H = 80
N = 128
Q = 256
KCONV = 4
LEN = 1024
DI = 5120
SEQS = 16


def steps_of(key, extent, shards, smallest, high):
    gain, own = 1.0, jax.random.fold_in(key, 6)
    for position, shards_of in shards:
        steps = jnp.exp(jax.random.uniform(jax.random.fold_in(own, position), (shards_of,), jnp.float32, smallest / len(shards), high / len(shards)))
        gain = gain * jnp.repeat(steps, extent[position] // shards_of).reshape([-1 if axis == position else 1 for axis in range(len(extent))])
    return gain


def normal_values(own_key, dims, scale, bound, split=(), kind=jnp.bfloat16):
    drawn = scale * jax.random.normal(own_key, dims, jnp.float32)
    if split:
        drawn = drawn * steps_of(own_key, dims, split, -0.22, 0.18)
    return jnp.clip(drawn, -bound, bound).astype(kind)


def setup_inputs(seed: int = 0) -> dict:
    seeds = jax.random.split(jax.random.key(seed), 17)
    tokens = normal_values(seeds[0], (LEN, SEQS, D), 1.0, 6.0, ((0, 2), (1, 16)))
    pre_gain = jnp.clip(1.0 + 0.15 * jax.random.normal(seeds[1], (D,), jnp.float32), 0.25, 1.75)
    z_weight = normal_values(seeds[2], (D, DI), D ** -0.5, 0.125, ((1, 2),))
    x_weight = normal_values(seeds[3], (D, DI), D ** -0.5, 0.125, ((1, 2),))
    bc_weight = normal_values(seeds[4], (D, 2 * N), D ** -0.5, 0.125)
    dt_weight = normal_values(seeds[5], (D, H), D ** -0.5, 0.125, ((1, 2),))
    conv_x_weight = normal_values(seeds[6], (KCONV, DI), KCONV ** -0.5, 3.0, ((1, 2),), jnp.float32)
    conv_x_bias = normal_values(seeds[7], (DI,), 0.5, 3.0, ((0, 2),), jnp.float32)
    conv_bc_weight = normal_values(seeds[8], (KCONV, 2 * N), KCONV ** -0.5, 3.0, (), jnp.float32)
    conv_bc_bias = normal_values(seeds[9], (2 * N,), 0.5, 3.0, (), jnp.float32)
    dt_bias = jnp.clip(-4.0 + 2.0 * jax.random.uniform(seeds[10], (H,), jnp.float32) ** steps_of(seeds[10], (H,), ((0, 2),), -0.2, 0.2), -4.0, -2.0)
    decay_log = jnp.clip(-6.0 + 6.0 * jax.random.uniform(seeds[11], (H,), jnp.float32) ** steps_of(seeds[11], (H,), ((0, 2),), -0.2, 0.2), -6.0, 0.0)
    skip_gain = jnp.clip(0.5 + 1.5 * jax.random.uniform(seeds[12], (H,), jnp.float32) ** steps_of(seeds[12], (H,), ((0, 2),), -0.2, 0.2), 0.5, 2.0)
    norm_gain = jnp.clip(1.0 + 0.15 * jax.random.normal(seeds[13], (DI,), jnp.float32), 0.25, 1.75)
    out_weight = normal_values(seeds[14], (DI, D), DI ** -0.5, 0.078125, ((0, 2),))
    cotangent = normal_values(seeds[15], (LEN, SEQS, D), 1.0, 6.0, ((0, 2), (1, 16)))
    return {"tokens": tokens, "pre_gain": pre_gain, "z_weight": z_weight, "x_weight": x_weight, "bc_weight": bc_weight, "dt_weight": dt_weight, "conv_x_weight": conv_x_weight, "conv_x_bias": conv_x_bias, "conv_bc_weight": conv_bc_weight, "conv_bc_bias": conv_bc_bias, "dt_bias": dt_bias, "decay_log": decay_log, "skip_gain": skip_gain, "norm_gain": norm_gain, "out_weight": out_weight, "cotangent": cotangent}


EPSILON = 1e-05
PRECISE = lax.Precision.HIGHEST

@jax.custom_vjp
def low(v):
    return lax.optimization_barrier(v.astype(jnp.bfloat16)).astype(jnp.float32)

@jax.custom_vjp
def low_back(v):
    return v

def low_keep(v):
    return (low(v), None)

def low_pass(kept, grad):
    return (grad,)

def back_keep(v):
    return (v, None)

def back_low(kept, grad):
    return (low(grad),)
low.defvjp(low_keep, low_pass)
low_back.defvjp(back_keep, back_low)

def rms_scale(values):
    return lax.rsqrt(lax.optimization_barrier(jnp.mean(values * values, axis=-1, keepdims=True)) + EPSILON)

def causal_conv(series, kernel, offsets):
    taps = kernel.shape[0]
    length = series.shape[0]
    padding = [(taps - 1, 0)] + [(0, 0)] * (series.ndim - 1)
    padded = jnp.pad(series, padding)
    summed = offsets + kernel[0] * padded[0:length]
    for tap_index in range(1, taps):
        summed = summed + kernel[tap_index] * padded[tap_index:tap_index + length]
    return jax.nn.silu(summed)

def state_space(inputs, steps, rates, b_proj, c_proj):
    length, heads, width = inputs.shape
    blocks = length // Q
    x_blocks = inputs.reshape(blocks, Q, heads, width)
    dt_blocks = steps.reshape(blocks, Q, heads)
    b_blocks = b_proj.reshape(blocks, Q, -1)
    c_blocks = c_proj.reshape(blocks, Q, -1)
    cumulative = jnp.cumsum(dt_blocks * rates, axis=1)
    by_head = jnp.transpose(cumulative, (0, 2, 1))
    spread = by_head[:, :, :, None] - by_head[:, :, None, :]
    causal = jnp.arange(Q)[:, None] >= jnp.arange(Q)[None, :]
    decay = jnp.exp(jnp.where(causal, spread, -jnp.inf))
    scores = jnp.einsum('kin,kjn->kij', c_blocks, b_blocks, precision=PRECISE)
    mixing = decay * scores[:, None] * jnp.transpose(dt_blocks, (0, 2, 1))[:, :, None, :]
    within = jnp.einsum('khij,kjhp->kihp', mixing, x_blocks, precision=PRECISE)
    to_end = jnp.exp(cumulative[:, -1:, :] - cumulative) * dt_blocks
    weighted = x_blocks * to_end[..., None]
    states = jnp.einsum('kjhp,kjn->khpn', weighted, b_blocks, precision=PRECISE)
    block_decay = jnp.exp(cumulative[:, -1, :])

    def advance(carried, element):
        factor, fresh = element
        return (carried * factor[:, None, None] + fresh, carried)
    _, entering = lax.scan(advance, jnp.zeros_like(states[0]), (block_decay, states))
    across = jnp.einsum('kin,khpn->kihp', c_blocks, entering, precision=PRECISE) * jnp.exp(cumulative)[..., None]
    return (within + across).reshape(length, heads, width)

def mixer_part(gate_in, x_in, b_proj, c_proj, dt_raw, conv_weight, conv_bias, dt_bias, decay_log, skip_gain):
    length = x_in.shape[0]
    heads = dt_bias.shape[0]
    conv_out = causal_conv(x_in, conv_weight, conv_bias).reshape(length, heads, -1)
    steps = jax.nn.softplus(dt_raw + dt_bias)
    result = state_space(conv_out, steps, -jnp.exp(decay_log), b_proj, c_proj) + skip_gain[:, None] * conv_out
    return result.reshape(length, -1) * jax.nn.silu(gate_in)

def dense(left, right):
    return jnp.dot(left, right, precision=PRECISE)

def layer(tokens, pre_gain, z_weight, x_weight, bc_weight, dt_weight, conv_x_weight, conv_x_bias, conv_bc_weight, conv_bc_bias, dt_bias, decay_log, skip_gain, norm_gain, out_weight):
    normed = low(tokens * rms_scale(tokens) * pre_gain)
    gate_in = low_back(dense(normed, z_weight))
    x_in = low_back(dense(normed, x_weight))
    bc_in = low_back(dense(normed, bc_weight))
    dt_raw = low_back(dense(normed, dt_weight))
    bc_conv = causal_conv(bc_in, conv_bc_weight, conv_bc_bias)
    mixed = mixer_part(gate_in, x_in, bc_conv[:, :N], bc_conv[:, N:], dt_raw, conv_x_weight, conv_x_bias, dt_bias, decay_log, skip_gain)
    gated = low(mixed * rms_scale(mixed) * norm_gain)
    return tokens + dense(gated, out_weight)

def reference(tokens, pre_gain, z_weight, x_weight, bc_weight, dt_weight, conv_x_weight, conv_x_bias, conv_bc_weight, conv_bc_bias, dt_bias, decay_log, skip_gain, norm_gain, out_weight, cotangent):
    params = tuple((item.astype(jnp.float32) for item in (pre_gain, z_weight, x_weight, bc_weight, dt_weight, conv_x_weight, conv_x_bias, conv_bc_weight, conv_bc_bias, dt_bias, decay_log, skip_gain, norm_gain, out_weight)))

    def one_sequence(grads, element):
        sequence, seq_grad = element
        result, back = jax.vjp(layer, sequence.astype(jnp.float32), *params)
        parts = back(seq_grad.astype(jnp.float32))
        grads = tuple((first + second for first, second in zip(grads, parts[1:])))
        return (grads, (result.astype(jnp.bfloat16), parts[0].astype(jnp.bfloat16)))
    zeros = tuple((jnp.zeros_like(item) for item in params))
    grads, (results, input_grads) = lax.scan(one_sequence, zeros, (jnp.moveaxis(tokens, 1, 0), jnp.moveaxis(cotangent, 1, 0)))
    return (jnp.moveaxis(results, 0, 1), jnp.moveaxis(input_grads, 0, 1), grads[0], grads[1], grads[2], grads[3], grads[4], grads[5], grads[6], grads[7], grads[8], grads[9], grads[10], grads[11], grads[12], grads[13])
```

```python
import jax
import jax.numpy as jnp
import numpy as np
from jax import lax
from jax.sharding import PartitionSpec as P

N = 128
Q = 256


EPSILON = 1e-05
PRECISE = lax.Precision.HIGHEST
BOTH = ("dp", "tensor")
F32 = jnp.float32
BF16 = jnp.bfloat16


def causal_conv(series, kernel, offsets):
    taps = kernel.shape[0]
    length = series.shape[0]
    padding = [(taps - 1, 0)] + [(0, 0)] * (series.ndim - 1)
    padded = jnp.pad(series, padding)
    summed = offsets + kernel[0] * padded[0:length]
    for tap_index in range(1, taps):
        summed = summed + kernel[tap_index] * padded[tap_index : tap_index + length]
    return jax.nn.silu(summed)


def state_space(inputs, steps, rates, b_proj, c_proj):
    length, heads, width = inputs.shape
    blocks = length // Q
    x_blocks = inputs.reshape(blocks, Q, heads, width)
    dt_blocks = steps.reshape(blocks, Q, heads)
    b_blocks = b_proj.reshape(blocks, Q, -1)
    c_blocks = c_proj.reshape(blocks, Q, -1)
    cumulative = jnp.cumsum(dt_blocks * rates, axis=1)
    by_head = jnp.transpose(cumulative, (0, 2, 1))
    spread = by_head[:, :, :, None] - by_head[:, :, None, :]
    causal = jnp.arange(Q)[:, None] >= jnp.arange(Q)[None, :]
    decay = jnp.exp(jnp.where(causal, spread, -jnp.inf))
    scores = jnp.einsum("kin,kjn->kij", c_blocks, b_blocks, precision=PRECISE)
    mixing = decay * scores[:, None] * jnp.transpose(dt_blocks, (0, 2, 1))[:, :, None, :]
    within = jnp.einsum("khij,kjhp->kihp", mixing, x_blocks, precision=PRECISE)
    to_end = jnp.exp(cumulative[:, -1:, :] - cumulative) * dt_blocks
    weighted = x_blocks * to_end[..., None]
    states = jnp.einsum("kjhp,kjn->khpn", weighted, b_blocks, precision=PRECISE)
    block_decay = jnp.exp(cumulative[:, -1, :])

    def advance(carried, element):
        factor, fresh = element
        return (carried * factor[:, None, None] + fresh, carried)

    _, entering = lax.scan(advance, jnp.zeros_like(states[0]), (block_decay, states))
    across = (
        jnp.einsum("kin,khpn->kihp", c_blocks, entering, precision=PRECISE)
        * jnp.exp(cumulative)[..., None]
    )
    return (within + across).reshape(length, heads, width)


def scan_part(x_in, b_proj, c_proj, dt_raw, conv_weight, conv_bias, dt_bias, decay_log, skip_gain):
    length = x_in.shape[0]
    heads = dt_bias.shape[0]
    conv_out = causal_conv(x_in, conv_weight, conv_bias).reshape(length, heads, -1)
    steps = jax.nn.softplus(dt_raw + dt_bias)
    result = (
        state_space(conv_out, steps, -jnp.exp(decay_log), b_proj, c_proj)
        + skip_gain[:, None] * conv_out
    )
    return result.reshape(length, -1)


def mm(a, b, dims, out=F32):
    return lax.dot_general(a, b, (dims, ((), ())), preferred_element_type=out)


def bit_orders(count):
    bits = count.bit_length() - 1
    rest = list(range(bits - 1, 1, -1))
    return [0, 1][:bits] + rest, [1, 0][-bits:] + rest if bits > 1 else [0]


def solution(mesh):
    count = mesh.shape["dp"]
    orders = bit_orders(count)
    levels = len(orders[0])
    tables = np.zeros((2, count), np.int32)
    for side in range(2):
        for place in range(count):
            tables[side, place] = sum(
                ((place >> (levels - 1 - k)) & 1) << orders[side][k] for k in range(levels)
            )
    swaps = []
    for k in range(levels):
        swaps.append(
            [
                (d * 2 + t, (d ^ (1 << orders[t][k])) * 2 + t)
                for d in range(count)
                for t in range(2)
            ]
        )
    flip = [(0, 1), (1, 0)]

    def other(value):
        return lax.ppermute(value, "tensor", flip)

    def pair_sum(value):
        return value + other(value)

    def level(k, values):
        half = values.shape[0] // 2
        came = lax.ppermute(values[half:].astype(BF16), BOTH, swaps[k])
        return values[:half] + came.astype(F32)

    def scatter_product(left, right):
        half = left.shape[0] // 2
        send = mm(left[half:], right, ((1,), (0,)), BF16)
        came = lax.ppermute(send, BOTH, swaps[0])
        keep = lax.optimization_barrier(mm(left[:half], right, ((1,), (0,))))
        total = keep + came.astype(F32)
        for k in range(1, levels):
            total = level(k, total)
        return total

    def body(
        tokens,
        pre_gain,
        z_weight,
        x_weight,
        bc_weight,
        dt_weight,
        conv_x_weight,
        conv_x_bias,
        conv_bc_weight,
        conv_bc_bias,
        dt_bias,
        decay_log,
        skip_gain,
        norm_gain,
        out_weight,
        cotangent,
    ):
        rows, _, width = tokens.shape
        inner_total = z_weight.shape[1] * 2
        me = lax.axis_index("dp")
        side = lax.axis_index("tensor")
        own_tokens = tokens[:, 0]
        own_grad = cotangent[:, 0]
        far_tokens = other(own_tokens)
        far_grad = other(own_grad)

        def join(own, far):
            return jnp.where(
                side == 0, jnp.concatenate([own, far], 0), jnp.concatenate([far, own], 0)
            )

        def own_half(value):
            return lax.dynamic_slice_in_dim(value, side * rows, rows, 0)

        def far_half(value):
            return lax.dynamic_slice_in_dim(value, (1 - side) * rows, rows, 0)

        grad_all = join(own_grad, far_grad)
        token_all = join(own_tokens, far_tokens).astype(F32)
        scale_all = lax.rsqrt(jnp.mean(token_all * token_all, axis=-1, keepdims=True) + EPSILON)
        normed = (token_all * scale_all * pre_gain).astype(BF16)

        places = jnp.where(side == 0, jnp.asarray(tables[0]), jnp.asarray(tables[1])) ^ me

        def travel_order(value):
            turned = lax.optimization_barrier(value.T).reshape(count, width // count, -1)
            return turned[places].reshape(width, -1)

        normed_turned = travel_order(normed)
        grad_turned = travel_order(grad_all)

        gate_in = mm(normed, z_weight, ((1,), (0,)))
        x_in = mm(normed, x_weight, ((1,), (0,)))
        bc_in = mm(normed, bc_weight, ((1,), (0,)))
        dt_raw = mm(normed, dt_weight, ((1,), (0,)))
        bc_conv, conv_back = jax.vjp(causal_conv, bc_in, conv_bc_weight, conv_bc_bias)
        y, scan_back = jax.vjp(
            scan_part,
            x_in,
            bc_conv[:, :N],
            bc_conv[:, N:],
            dt_raw,
            conv_x_weight,
            conv_x_bias,
            dt_bias,
            decay_log,
            skip_gain,
        )
        sig = jax.nn.sigmoid(gate_in)
        mixed = y * gate_in * sig
        squares = pair_sum(jnp.sum(mixed * mixed, axis=-1, keepdims=True))
        gate_scale = lax.rsqrt(squares / inner_total + EPSILON)
        gated = (mixed * gate_scale * norm_gain).astype(BF16)
        grad_out = scatter_product(grad_turned, gated).T

        d_gated = mm(grad_all, out_weight, ((1,), (1,)))
        grad_norm = jnp.sum(d_gated * mixed * gate_scale, axis=0)
        scaled = d_gated * norm_gain
        inner_dot = pair_sum(jnp.sum(scaled * mixed, axis=-1, keepdims=True))
        d_mixed = gate_scale * scaled - mixed * gate_scale**3 * inner_dot / inner_total
        low_gate = (d_mixed * y * sig * (1.0 + gate_in * (1.0 - sig))).astype(BF16)
        grad_z = scatter_product(normed_turned, low_gate)

        far_branch = other(mm(far_half(gated), out_weight, ((1,), (0,)), BF16))
        own_branch = mm(own_half(gated), out_weight, ((1,), (0,)))
        token_f = own_tokens.astype(F32)
        layer_out = (token_f + own_branch + far_branch.astype(F32)).astype(BF16)

        (
            grad_x_in,
            grad_b,
            grad_c,
            grad_dt,
            grad_conv_w,
            grad_conv_b,
            grad_dt_bias,
            grad_decay,
            grad_skip,
        ) = scan_back(d_mixed * gate_in * sig)
        low_x = grad_x_in.astype(BF16)
        grad_xw = scatter_product(normed_turned, low_x)
        grad_bc_conv = pair_sum(jnp.concatenate([grad_b, grad_c], axis=-1))
        grad_bc_in, grad_conv_bc_w, grad_conv_bc_b = conv_back(grad_bc_conv)
        low_bc = grad_bc_in.astype(BF16)
        low_dt = grad_dt.astype(BF16)
        half_bc = lax.dynamic_slice_in_dim(low_bc, side * N, N, 1)
        grad_small = scatter_product(
            normed_turned,
            jnp.concatenate([half_bc, low_dt], axis=-1),
        )
        own_bcw = grad_small[:, :N]
        far_bcw = other(own_bcw)
        grad_bcw = jnp.where(
            side == 0,
            jnp.concatenate([own_bcw, far_bcw], 1),
            jnp.concatenate([far_bcw, own_bcw], 1),
        )
        grad_dtw = grad_small[:, N:]

        def back(part):
            return (
                mm(part(low_gate), z_weight, ((1,), (1,)))
                + mm(part(low_x), x_weight, ((1,), (1,)))
                + mm(part(low_dt), dt_weight, ((1,), (1,)))
            )

        far_back = other(back(far_half))
        d_normed = back(own_half) + mm(own_half(low_bc), bc_weight, ((1,), (1,))) + far_back
        pre_scale = own_half(scale_all)
        grad_pre = lax.psum(jnp.sum(d_normed * token_f * pre_scale, axis=0), BOTH)
        gained = d_normed * pre_gain
        grad_tokens = (
            own_grad.astype(F32)
            + pre_scale * gained
            - token_f * pre_scale**3 * jnp.mean(gained * token_f, axis=-1, keepdims=True)
        )
        (
            grad_norm,
            grad_conv_w,
            grad_conv_b,
            grad_conv_bc_w,
            grad_conv_bc_b,
            grad_dt_bias,
            grad_decay,
            grad_skip,
        ) = lax.psum(
            (
                grad_norm,
                grad_conv_w,
                grad_conv_b,
                grad_conv_bc_w,
                grad_conv_bc_b,
                grad_dt_bias,
                grad_decay,
                grad_skip,
            ),
            "dp",
        )
        return (
            layer_out[:, None],
            grad_tokens.astype(BF16)[:, None],
            grad_pre,
            grad_z,
            grad_xw,
            grad_bcw,
            grad_dtw,
            grad_conv_w,
            grad_conv_b,
            grad_conv_bc_w,
            grad_conv_bc_b,
            grad_dt_bias,
            grad_decay,
            grad_skip,
            grad_norm,
            grad_out,
        )

    in_specs = (
        P("tensor", "dp", None),
        P(),
        P(None, "tensor"),
        P(None, "tensor"),
        P(),
        P(None, "tensor"),
        P(None, "tensor"),
        P("tensor"),
        P(),
        P(),
        P("tensor"),
        P("tensor"),
        P("tensor"),
        P("tensor"),
        P("tensor", None),
        P("tensor", "dp", None),
    )
    out_specs = (
        P("tensor", "dp", None),
        P("tensor", "dp", None),
        P(),
        P("dp", "tensor"),
        P("dp", "tensor"),
        P("dp", None),
        P("dp", "tensor"),
        P(None, "tensor"),
        P("tensor"),
        P(),
        P(),
        P("tensor"),
        P("tensor"),
        P("tensor"),
        P("tensor"),
        P("tensor", "dp"),
    )
    return jax.shard_map(body, mesh=mesh, in_specs=in_specs, out_specs=out_specs, check_vma=False)
```
